256 devices in a mesh: wide: 32 (over y, x, core), narrow: 8 (over z).
Axes of the slice: x: 4, y: 4, z: 8, core: 2. Of those that a mesh axis runs over, the one named last changes fastest.
Arguments:
- three_centre: float32 [128, 2048, 1024], P(None, 'wide', 'narrow'), may hold values from -6 to 6
- screen_mask: int32 [128, 16, 8], P('wide', None, 'narrow'), may hold values 0 or 1
- metric: bfloat16 [1024, 1024], P(None, 'narrow'), may hold values from -0.1875 to 0.1875
Outputs:
- contracted: float32 [128, 2048, 1024], P('wide', None, 'narrow')
The draws below stay inside these ranges and needn't reach their ends.
All inputs are finite; a program needn't handle non-finite values. No bound on the sum of `screen_mask` on one device may be relied on, other than what follows from the above.
Results may differ from the reference program's by a relative error of at most 0.0029.
Values may be sent and summed in bfloat16 or wider, within the bound.
A program may use at most 64 MiB of HBM per device.

```python
import jax
import jax.numpy as jnp
from jax import lax

BLK = 128
NUB = 16
AUXB = 8
MU = 128
NU = 2048
AUX = 1024


def place_ends(drawn, own_key, least, largest):
    longest = drawn.shape.index(max(drawn.shape))
    spots = []
    for shift in (0, 1):
        where = [jax.random.randint(jax.random.fold_in(own_key, axis), (), 0, length) for axis, length in enumerate(drawn.shape)]
        where[longest] = (where[longest] + shift) % drawn.shape[longest]
        spots.append(tuple(where))
    return drawn.at[spots[0]].set(least).at[spots[1]].set(largest)


def level_of(rng, extent, split, smallest, top_value):
    factor_of, own = 1.0, jax.random.fold_in(rng, 6)
    for axis_at, parts in split:
        steps = jnp.exp(jax.random.uniform(jax.random.fold_in(own, axis_at), (parts,), jnp.float32, smallest / len(split), top_value / len(split)))
        factor_of = factor_of * jnp.repeat(steps, extent[axis_at] // parts).reshape([-1 if axis == axis_at else 1 for axis in range(len(extent))])
    return factor_of


def centred(stream_key, shape, width, limit, split=(), kind=jnp.bfloat16):
    gain = level_of(stream_key, shape, split, -0.22, 0.18) if split else 1.0
    drawn = jax.random.normal(stream_key, shape, jnp.float32) * width * gain
    return jnp.minimum(jnp.maximum(drawn, -limit), limit).astype(kind)


def setup_inputs(seed: int = 0) -> dict:
    key_list = jax.random.split(jax.random.key(seed), 4)
    three_centre = centred(key_list[0], (MU, NU, AUX), 1.0, 6.0, ((1, 32), (2, 8)), jnp.float32)
    screen_mask = place_ends((jax.random.randint(key_list[1], (MU, NUB, AUXB), 0, 3) < 2).astype(jnp.int32), jax.random.fold_in(key_list[1], 1), 0, 1)
    metric = centred(key_list[2], (AUX, AUX), AUX ** -0.5, 0.1875, ((1, 8),))
    return {"three_centre": three_centre, "screen_mask": screen_mask, "metric": metric}


def reference(three_centre, screen_mask, metric):
    def one_row(operands):
        slab, row_mask = operands
        blocks = slab.reshape(NUB, BLK, AUXB, BLK)
        weights = row_mask[:, None, :, None].astype(jnp.float32)
        screened = (blocks * weights).reshape(NU, AUX).astype(jnp.bfloat16)
        return jnp.dot(screened, metric, preferred_element_type=jnp.float32)

    return lax.map(one_row, (three_centre, screen_mask))
```

```python
import jax
import jax.numpy as jnp
from jax import lax
from jax.experimental import pallas as pl
from jax.experimental.pallas import tpu as pltpu
from jax.sharding import PartitionSpec as P

MESH = pl.DeviceIdType.MESH
BF = jnp.bfloat16
F32 = jnp.float32
SIDE, CORES, DEPTH = 4, 2, 8
WIDE = SIDE * SIDE * CORES
CHIPS = SIDE * SIDE
LANES = 128
PAIR = 2

OFFSETS = (
    (0, 0), (1, 0), (-1, 0), (0, 1), (0, -1), (1, 1), (-1, -1), (-1, 1),
    (1, -1), (2, 0), (0, 2), (2, 1), (1, 2), (2, -1), (-1, 2), (2, 2),
)
Z_ORDER = (4, 3, 5, 2, 6, 1, 7)
METRIC_FROM = 4


def pick(index, table):
    total = jnp.int32(0)
    for k, value in enumerate(table):
        if value:
            total = total + jnp.where(index == k, jnp.int32(value), jnp.int32(0))
    return total


def body(
    x_ref, mask_ref, metric_ref, out_ref,
    xf, xb, rb, sb, ab, mb, yb,
    load_sem, own_sem, s1_send, s1_recv, a_send, a_recv, b_send, b_recv,
    mz_send, mz_recv, mm_send, mm_recv, mc_send, mc_recv,
):
    w = lax.axis_index("wide")
    z = lax.axis_index("narrow")
    core = lax.rem(w, 2)
    xx = lax.rem(w // 2, SIDE)
    yy = w // (2 * SIDE)
    half, quarter = z // 4, lax.rem(z, 4)

    def chip_at(dx, dy):
        return lax.rem(yy + dy + SIDE, SIDE) * SIDE + lax.rem(xx + dx + SIDE, SIDE)

    def load(g):
        dx, dy = OFFSETS[g]
        rows = pl.ds(chip_at(dx, dy) * 8, 8)
        return pltpu.make_async_copy(x_ref.at[rows], xf.at[rows], load_sem.at[g])

    for g in range(CHIPS):
        load(g).start()

    barrier = pltpu.get_barrier_semaphore()
    for k in range(1, DEPTH):
        pl.semaphore_signal(
            barrier, inc=1, device_id=(w, lax.rem(z + k, DEPTH)), device_id_type=MESH
        )
    for g in range(CHIPS):
        dx, dy = OFFSETS[g]
        for dc in (0, 1):
            if g == 0 and dc == 0:
                continue
            pl.semaphore_signal(
                barrier, inc=1,
                device_id=(chip_at(dx, dy) * 2 + lax.rem(core + dc, 2), z),
                device_id_type=MESH,
            )

    def convert(g):
        dx, dy = OFFSETS[g]
        first = chip_at(dx, dy) * 8
        load(g).wait()
        xb[pl.ds(first, 8)] = xf[pl.ds(first, 8)].astype(BF)

    convert(0)
    convert(1)
    pl.semaphore_wait(barrier, DEPTH - 1 + WIDE - 1)

    my_rows = pl.ds(pl.multiple_of(w * 32, 32), 32)
    my_lanes = pl.ds(pl.multiple_of(z * LANES, LANES), LANES)
    pltpu.make_async_copy(metric_ref.at[my_rows], mb.at[w, :, my_lanes], mz_recv).start()
    for k in Z_ORDER:
        pltpu.make_async_remote_copy(
            metric_ref.at[my_rows], mb.at[w, :, my_lanes], mz_send, mz_recv,
            device_id=(w, lax.rem(z + k, DEPTH)), device_id_type=MESH,
        ).start()

    def plane_send(g):
        dx, dy = OFFSETS[g]
        chip = chip_at(dx, dy)
        if g == 0:
            pltpu.make_async_copy(xb.at[pl.ds(w * 4, 4)], rb.at[0, core], s1_recv.at[0]).start()
        for dc in (0, 1):
            if g == 0 and dc == 0:
                continue
            there = chip * 2 + lax.rem(core + dc, 2)
            pltpu.make_async_remote_copy(
                xb.at[pl.ds(there * 4, 4)], rb.at[g, core], s1_send, s1_recv.at[g],
                device_id=(there, z), device_id_type=MESH,
            ).start()

    def metric_send(g):
        dx, dy = OFFSETS[g]
        pltpu.make_async_remote_copy(
            mb.at[w], mb.at[w], mm_send, mm_recv.at[g],
            device_id=(chip_at(dx, dy) * 2 + core, z), device_id_type=MESH,
        ).start()

    def metric_across(source):
        pltpu.make_async_remote_copy(
            mb.at[source], mb.at[source], mc_send, mc_recv,
            device_id=(w + 1 - 2 * core, z), device_id_type=MESH,
        ).start()

    for g in range(CHIPS):
        if g + 2 < CHIPS:
            convert(g + 2)
        plane_send(g)
        if g == METRIC_FROM:
            pltpu.make_async_copy(mb.at[w], mb.at[w], mz_recv).wait()
            metric_across(w)
        if g > METRIC_FROM:
            metric_send(g - METRIC_FROM)
    for g in range(CHIPS - METRIC_FROM, CHIPS):
        metric_send(g)

    def screen(g):
        dx, dy = OFFSETS[g]
        chip = chip_at(-dx, -dy)
        pltpu.make_async_copy(rb.at[g], rb.at[g], s1_recv.at[g]).wait()
        for m in range(4):
            weight = mask_ref[m, chip].astype(F32)
            for c in range(CORES):
                piece = (rb[g, c, m].astype(F32) * weight).astype(BF)
                sb[g, pl.ds((m // 2) * 4, 4), m % 2, c] = piece.reshape(4, 16, LANES)

    def deep_send(g):
        pltpu.make_async_copy(sb.at[g, z], ab.at[g, :, :, :, my_lanes], a_recv.at[g]).start()
        for k in Z_ORDER:
            there = lax.rem(z + k, DEPTH)
            pltpu.make_async_remote_copy(
                sb.at[g, there], ab.at[g, :, :, :, my_lanes], a_send, a_recv.at[g],
                device_id=(w, there), device_id_type=MESH,
            ).start()

    for g in range(CHIPS):
        screen(g)
        if g >= 1:
            deep_send(g - 1)
        if g > METRIC_FROM:
            k = g - METRIC_FROM
            dx, dy = OFFSETS[k]
            source = chip_at(-dx, -dy) * 2 + core
            pltpu.make_async_copy(mb.at[source], mb.at[source], mm_recv.at[k]).wait()
            metric_across(source)
    deep_send(CHIPS - 1)
    for k in range(CHIPS - METRIC_FROM, CHIPS):
        dx, dy = OFFSETS[k]
        source = chip_at(-dx, -dy) * 2 + core
        pltpu.make_async_copy(mb.at[source], mb.at[source], mm_recv.at[k]).wait()
        metric_across(source)
    pltpu.make_async_copy(mb.at[pl.ds(0, CHIPS)], mb.at[pl.ds(0, CHIPS)], mc_recv).wait()

    dxs = [dx % SIDE for dx, _ in OFFSETS]
    dys = [dy % SIDE for _, dy in OFFSETS]

    def result_send(g):
        xs = lax.rem(xx - pick(g, dxs) + SIDE, SIDE)
        ys = lax.rem(yy - pick(g, dys) + SIDE, SIDE)
        place = out_ref.at[pl.ds(half * 2, 2), ys, xs, :, quarter]
        pltpu.make_async_copy(yb.at[g, :, :, :, my_lanes], place, b_recv).start()
        for k in Z_ORDER:
            there = lax.rem(z + k, DEPTH)
            lanes = pl.ds(pl.multiple_of(there * LANES, LANES), LANES)
            pltpu.make_async_remote_copy(
                yb.at[g, :, :, :, lanes], place, b_send, b_recv,
                device_id=(w, there), device_id_type=MESH,
            ).start()

    def contract(step):
        for i in range(PAIR):
            g = step * PAIR + i
            pltpu.make_async_copy(ab.at[g], ab.at[g], a_recv.at[g]).wait()
        rows = ab[pl.ds(step * PAIR, PAIR)].reshape(PAIR * 64, 1024)
        product = jnp.dot(rows, mb[...].reshape(1024, 1024), preferred_element_type=F32)
        yb[pl.ds(step * PAIR, PAIR)] = product.astype(BF).reshape(PAIR, 2, 2, 16, 1024)

    contract(0)

    @pl.loop(1, CHIPS // PAIR)
    def _(step):
        contract(step)
        for i in range(PAIR):
            result_send((step - 1) * PAIR + i)

    for i in range(PAIR):
        result_send(CHIPS - PAIR + i)

    def drain(ref, sem):
        pltpu.make_async_copy(ref, ref, sem).wait()

    drain(xb.at[pl.ds(0, 124)], s1_send)
    drain(mb.at[0, :, pl.ds(0, 7 * LANES)], mz_send)
    drain(mb.at[pl.ds(0, 15)], mm_send)
    drain(mb.at[pl.ds(0, 16)], mc_send)
    drain(sb.at[:, pl.ds(0, 7)], a_send)
    drain(yb.at[:, :, :, :, pl.ds(0, 7 * LANES)], b_send)
    drain(out_ref, b_recv)


def per_device(three_centre, screen_mask, metric):
    dma = pltpu.SemaphoreType.DMA
    result = pl.pallas_call(
        body,
        out_shape=jax.ShapeDtypeStruct((4, SIDE, SIDE, CORES, 4, 16, LANES), BF),
        in_specs=[
            pl.BlockSpec(memory_space=pl.ANY),
            pl.BlockSpec(memory_space=pltpu.SMEM),
            pl.BlockSpec(memory_space=pl.ANY),
        ],
        out_specs=pl.BlockSpec(memory_space=pl.ANY),
        scratch_shapes=[
            pltpu.VMEM((128, 64, LANES), F32),
            pltpu.VMEM((128, 64, LANES), BF),
            pltpu.VMEM((CHIPS, CORES, 4, 64, LANES), BF),
            pltpu.VMEM((CHIPS, DEPTH, 2, 2, 16, LANES), BF),
            pltpu.VMEM((CHIPS, 2, 2, 16, 1024), BF),
            pltpu.VMEM((WIDE, 32, 1024), BF),
            pltpu.VMEM((CHIPS, 2, 2, 16, 1024), BF),
            dma((CHIPS,)), dma, dma, dma((CHIPS,)), dma, dma((CHIPS,)), dma, dma,
            dma, dma, dma, dma((CHIPS,)), dma, dma,
        ],
        compiler_params=pltpu.CompilerParams(
            collective_id=0, has_side_effects=True, vmem_limit_bytes=56 * 1024 * 1024
        ),
        name="screen_contract",
    )(three_centre, screen_mask.reshape(4, 16), metric)
    return result.reshape(4, 2048, LANES).astype(F32)


def solution(mesh):
    in_specs = (P(None, "wide", "narrow"), P("wide", None, "narrow"), P(None, "narrow"))
    out_specs = P("wide", None, "narrow")
    return jax.shard_map(
        per_device, mesh=mesh, in_specs=in_specs, out_specs=out_specs, check_vma=False
    )
```

```python
import jax
import jax.numpy as jnp
from jax import lax
from jax.experimental import pallas as pl
from jax.experimental.pallas import tpu as pltpu
from jax.sharding import PartitionSpec as P

MESH = pl.DeviceIdType.MESH
BF = jnp.bfloat16
F32 = jnp.float32
SIDE, CORES, DEPTH = 4, 2, 8
WIDE = SIDE * SIDE * CORES
CHIPS = SIDE * SIDE
LANES = 128
PAIR = 2

OFFSETS = (
    (0, 0), (1, 0), (-1, 0), (0, 1), (0, -1), (1, 1), (-1, -1), (-1, 1),
    (1, -1), (2, 0), (0, 2), (2, 1), (1, 2), (2, -1), (-1, 2), (2, 2),
)
Z_ORDER = (4, 3, 5, 2, 6, 1, 7)
METRIC_FROM = 8
NEAR = 4
EARLY = 8
UNITS_FROM = 9


def pick(index, table):
    total = jnp.int32(0)
    for k, value in enumerate(table):
        if value:
            total = total + jnp.where(index == k, jnp.int32(value), jnp.int32(0))
    return total


def body(
    x_ref, mask_ref, metric_ref, out_ref,
    ob, xf, xb, rb, sb, ab, mb, yb,
    load_sem, own_sem, s1_send, s1_recv, a_send, a_recv, b_send, b_recv,
    mz_send, mz_recv, mm_send, mm_recv, mc_send, mc_recv,
):
    w = lax.axis_index("wide")
    z = lax.axis_index("narrow")
    core = lax.rem(w, 2)
    xx = lax.rem(w // 2, SIDE)
    yy = w // (2 * SIDE)
    half, quarter = z // 4, lax.rem(z, 4)

    def chip_at(dx, dy):
        return lax.rem(yy + dy + SIDE, SIDE) * SIDE + lax.rem(xx + dx + SIDE, SIDE)

    def load(g):
        dx, dy = OFFSETS[g]
        rows = pl.ds(chip_at(dx, dy) * 8, 8)
        return pltpu.make_async_copy(x_ref.at[rows], xf.at[rows], load_sem.at[g])

    barrier = pltpu.get_barrier_semaphore()
    for k in Z_ORDER:
        pl.semaphore_signal(
            barrier, inc=1, device_id=(w, lax.rem(z + k, DEPTH)), device_id_type=MESH
        )
    for g in range(CHIPS - 1, -1, -1):
        dx, dy = OFFSETS[g]
        for dc in (0, 1):
            if g == 0 and dc == 0:
                continue
            pl.semaphore_signal(
                barrier, inc=1,
                device_id=(chip_at(dx, dy) * 2 + lax.rem(core + dc, 2), z),
                device_id_type=MESH,
            )

    for g in range(CHIPS):
        load(g).start()

    def convert(g):
        dx, dy = OFFSETS[g]
        first = chip_at(dx, dy) * 8
        load(g).wait()
        xb[pl.ds(first, 8)] = xf[pl.ds(first, 8)].astype(BF)

    def masked(block, weight):
        return (block.astype(F32) * weight).astype(BF).reshape(4, 16, LANES)

    for g in range(EARLY):
        convert(g)
    for m in range(4):
        weight = mask_ref[m, w // 2].astype(F32)
        sb[0, pl.ds((m // 2) * 4, 4), m % 2, core] = masked(xb[w * 4 + m], weight)
    pl.semaphore_wait(barrier, DEPTH - 1 + WIDE - 1)

    my_lanes = pl.ds(pl.multiple_of(z * LANES, LANES), LANES)

    def deep_send(g, cores=slice(None)):
        place = ab.at[g, :, cores, :, my_lanes]
        for k in Z_ORDER:
            there = lax.rem(z + k, DEPTH)
            pltpu.make_async_remote_copy(
                sb.at[g, there, :, cores], place, a_send, a_recv.at[g],
                device_id=(w, there), device_id_type=MESH,
            ).start()
        pltpu.make_async_copy(sb.at[g, z, :, cores], place, a_recv.at[g]).start()

    deep_send(0, pl.ds(core, 1))

    my_rows = pl.ds(pl.multiple_of(w * 32, 32), 32)

    def metric_start():
        pltpu.make_async_copy(metric_ref.at[my_rows], mb.at[w, :, my_lanes], mz_recv).start()
        for k in Z_ORDER:
            pltpu.make_async_remote_copy(
                metric_ref.at[my_rows], mb.at[w, :, my_lanes], mz_send, mz_recv,
                device_id=(w, lax.rem(z + k, DEPTH)), device_id_type=MESH,
            ).start()

    def plane_send(g, dc):
        dx, dy = OFFSETS[g]
        there = chip_at(dx, dy) * 2 + lax.rem(core + dc, 2)
        pltpu.make_async_remote_copy(
            xb.at[pl.ds(there * 4, 4)], rb.at[g, core], s1_send, s1_recv.at[g, core],
            device_id=(there, z), device_id_type=MESH,
        ).start()

    def metric_send(g):
        dx, dy = OFFSETS[g]
        pltpu.make_async_remote_copy(
            mb.at[w], mb.at[w], mm_send, mm_recv.at[g],
            device_id=(chip_at(dx, dy) * 2 + core, z), device_id_type=MESH,
        ).start()

    def metric_across(source):
        pltpu.make_async_remote_copy(
            mb.at[source], mb.at[source], mc_send, mc_recv,
            device_id=(w + 1 - 2 * core, z), device_id_type=MESH,
        ).start()

    def screen(g, dc):
        dx, dy = OFFSETS[g]
        chip = chip_at(-dx, -dy)
        c = lax.rem(core + dc, 2)
        arrived = rb.at[g, c]
        pltpu.make_async_copy(arrived, arrived, s1_recv.at[g, c]).wait()
        for m in range(4):
            weight = mask_ref[m, chip].astype(F32)
            sb[g, pl.ds((m // 2) * 4, 4), m % 2, c] = masked(rb[g, c, m], weight)

    def core_send(g, dc):
        deep_send(g, pl.ds(lax.rem(core + dc, 2), 1))

    def metric_arrived(k):
        dx, dy = OFFSETS[k]
        source = chip_at(-dx, -dy) * 2 + core
        pltpu.make_async_copy(mb.at[source], mb.at[source], mm_recv.at[k]).wait()
        metric_across(source)

    units = [(g, dc) for dc in (0, 1) for g in range(1, NEAR + 1)]
    units_all = list(units)
    pending = []
    plane_send(0, 1)
    for g, dc in units:
        plane_send(g, dc)
    metric_start()
    screen(0, 1)
    for g in range(NEAR + 1, CHIPS):
        if g >= EARLY:
            convert(g)
        plane_send(g, 0)
        plane_send(g, 1)
        if g == NEAR + 1:
            core_send(0, 1)
        if g == METRIC_FROM:
            pltpu.make_async_copy(mb.at[w], mb.at[w], mz_recv).wait()
            metric_across(w)
        if g > METRIC_FROM:
            metric_send(g - METRIC_FROM)
        if g > UNITS_FROM and units:
            screen(*units.pop(0))
            pending.append(units_all.pop(0))
            if len(pending) > 1:
                core_send(*pending.pop(0))
    for g in range(CHIPS - METRIC_FROM, CHIPS):
        metric_send(g)
    for unit in units:
        screen(*unit)
        pending.append(unit)
        core_send(*pending.pop(0))
    for g in range(NEAR + 1, CHIPS):
        screen(g, 0)
        screen(g, 1)
        if g == NEAR + 1:
            core_send(*pending.pop(0))
        else:
            deep_send(g - 1)
        if g > METRIC_FROM:
            metric_arrived(g - METRIC_FROM)
    deep_send(CHIPS - 1)
    for k in range(CHIPS - METRIC_FROM, CHIPS):
        metric_arrived(k)
    pltpu.make_async_copy(mb.at[pl.ds(0, CHIPS)], mb.at[pl.ds(0, CHIPS)], mc_recv).wait()

    dxs = [dx % SIDE for dx, _ in OFFSETS]
    dys = [dy % SIDE for _, dy in OFFSETS]

    def result_send(g):
        xs = lax.rem(xx - pick(g, dxs) + SIDE, SIDE)
        ys = lax.rem(yy - pick(g, dys) + SIDE, SIDE)
        place = ob.at[pl.ds(half * 2, 2), ys, xs, :, quarter]
        pltpu.make_async_copy(yb.at[g, :, :, :, my_lanes], place, b_recv.at[g]).start()
        for k in Z_ORDER:
            there = lax.rem(z + k, DEPTH)
            lanes = pl.ds(pl.multiple_of(there * LANES, LANES), LANES)
            pltpu.make_async_remote_copy(
                yb.at[g, :, :, :, lanes], place, b_send, b_recv.at[g],
                device_id=(w, there), device_id_type=MESH,
            ).start()

    def contract(step):
        for i in range(PAIR):
            g = step * PAIR + i
            pltpu.make_async_copy(ab.at[g], ab.at[g], a_recv.at[g]).wait()
        rows = ab[pl.ds(step * PAIR, PAIR)].reshape(PAIR * 64, 1024)
        product = jnp.dot(rows, mb[...].reshape(1024, 1024), preferred_element_type=F32)
        yb[pl.ds(step * PAIR, PAIR)] = product.astype(BF).reshape(PAIR, 2, 2, 16, 1024)

    contract(0)

    @pl.loop(1, CHIPS // PAIR)
    def _(step):
        contract(step)
        for i in range(PAIR):
            result_send((step - 1) * PAIR + i)

    for i in range(PAIR):
        result_send(CHIPS - PAIR + i)

    def drain(ref, sem):
        pltpu.make_async_copy(ref, ref, sem).wait()

    drain(xb.at[pl.ds(0, 124)], s1_send)
    drain(mb.at[0, :, pl.ds(0, 7 * LANES)], mz_send)
    drain(mb.at[pl.ds(0, 15)], mm_send)
    drain(mb.at[pl.ds(0, 16)], mc_send)
    drain(sb.at[:, pl.ds(0, 7)], a_send)
    drain(yb.at[:, :, :, :, pl.ds(0, 7 * LANES)], b_send)

    @pl.loop(0, CHIPS)
    def _(g):
        xs = lax.rem(xx - pick(g, dxs) + SIDE, SIDE)
        ys = lax.rem(yy - pick(g, dys) + SIDE, SIDE)
        landed = ob.at[:, ys, xs]
        pltpu.make_async_copy(landed, landed, b_recv.at[g]).wait()
        out_ref[:, ys, xs] = landed[...].astype(F32)


def per_device(three_centre, screen_mask, metric):
    dma = pltpu.SemaphoreType.DMA
    result = pl.pallas_call(
        body,
        out_shape=pltpu.VMEM((4, SIDE, SIDE, CORES, 4, 16, LANES), F32),
        in_specs=[
            pl.BlockSpec(memory_space=pl.ANY),
            pl.BlockSpec(memory_space=pltpu.SMEM),
            pl.BlockSpec(memory_space=pl.ANY),
        ],
        out_specs=pl.BlockSpec(memory_space=pltpu.VMEM),
        scratch_shapes=[
            pltpu.VMEM((4, SIDE, SIDE, CORES, 4, 16, LANES), BF),
            pltpu.VMEM((128, 64, LANES), F32),
            pltpu.VMEM((128, 64, LANES), BF),
            pltpu.VMEM((CHIPS, CORES, 4, 64, LANES), BF),
            pltpu.VMEM((CHIPS, DEPTH, 2, 2, 16, LANES), BF),
            pltpu.VMEM((CHIPS, 2, 2, 16, 1024), BF),
            pltpu.VMEM((WIDE, 32, 1024), BF),
            pltpu.VMEM((CHIPS, 2, 2, 16, 1024), BF),
            dma((CHIPS,)), dma, dma, dma((CHIPS, CORES)), dma, dma((CHIPS,)), dma, dma((CHIPS,)),
            dma, dma, dma, dma((CHIPS,)), dma, dma,
        ],
        compiler_params=pltpu.CompilerParams(
            collective_id=0, has_side_effects=True, vmem_limit_bytes=56 * 1024 * 1024
        ),
        name="screen_contract",
    )(three_centre, screen_mask.reshape(4, 16), metric)
    return result.reshape(4, 2048, LANES)


def solution(mesh):
    in_specs = (P(None, "wide", "narrow"), P("wide", None, "narrow"), P(None, "narrow"))
    out_specs = P("wide", None, "narrow")
    return jax.shard_map(
        per_device, mesh=mesh, in_specs=in_specs, out_specs=out_specs, check_vma=False
    )
```

```python
import jax
import jax.numpy as jnp
from jax import lax
from jax.experimental import pallas as pl
from jax.experimental.pallas import tpu as pltpu
from jax.sharding import PartitionSpec as P

MESH = pl.DeviceIdType.MESH
BF = jnp.bfloat16
F32 = jnp.float32
SIDE, CORES, DEPTH = 4, 2, 8
WIDE = SIDE * SIDE * CORES
CHIPS = SIDE * SIDE
LANES = 128
PAIR = 2

OFFSETS = (
    (0, 0), (1, 0), (-1, 0), (0, 1), (0, -1), (1, 1), (-1, -1), (-1, 1),
    (1, -1), (2, 0), (0, 2), (2, 1), (1, 2), (2, -1), (-1, 2), (2, 2),
)
Z_ORDER = (4, 3, 5, 2, 6, 1, 7)
METRIC_FROM = 8
NEAR = 4
FURTHER = (5, 11, 15)
EARLY = 8
UNITS_FROM = 9


def pick(index, table):
    total = jnp.int32(0)
    for k, value in enumerate(table):
        if value:
            total = total + jnp.where(index == k, jnp.int32(value), jnp.int32(0))
    return total


def body(
    x_ref, mask_ref, metric_ref, out_ref,
    ob, xf, xb, rb, sb, ab, mb, yb,
    load_sem, own_sem, s1_send, s1_recv, a_send, a_recv, b_send, b_recv,
    mz_send, mz_recv, mm_send, mm_recv, mc_send, mc_recv, rounds,
):
    w = lax.axis_index("wide")
    z = lax.axis_index("narrow")
    core = lax.rem(w, 2)
    xx = lax.rem(w // 2, SIDE)
    yy = w // (2 * SIDE)
    half, quarter = z // 4, lax.rem(z, 4)

    def chip_at(dx, dy):
        return lax.rem(yy + dy + SIDE, SIDE) * SIDE + lax.rem(xx + dx + SIDE, SIDE)

    def load(g):
        dx, dy = OFFSETS[g]
        rows = pl.ds(chip_at(dx, dy) * 8, 8)
        return pltpu.make_async_copy(x_ref.at[rows], xf.at[rows], load_sem.at[g])

    barrier = pltpu.get_barrier_semaphore()
    for k in Z_ORDER:
        pl.semaphore_signal(
            barrier, inc=1, device_id=(w, lax.rem(z + k, DEPTH)), device_id_type=MESH
        )
    for g in range(NEAR, -1, -1):
        dx, dy = OFFSETS[g]
        for dc in (0, 1):
            if g == 0 and dc == 0:
                continue
            pl.semaphore_signal(
                barrier, inc=1,
                device_id=(chip_at(dx, dy) * 2 + lax.rem(core + dc, 2), z),
                device_id_type=MESH,
            )

    def tell(r):
        for g in range(1, NEAR + 1):
            pl.semaphore_signal(
                rounds.at[r - 1], inc=1,
                device_id=(chip_at(*OFFSETS[g]) * 2 + core, z), device_id_type=MESH,
            )

    def hear(r):
        pl.semaphore_wait(rounds.at[r - 1], 4)

    for g in range(CHIPS):
        load(g).start()

    def convert(g):
        dx, dy = OFFSETS[g]
        first = chip_at(dx, dy) * 8
        load(g).wait()
        xb[pl.ds(first, 8)] = xf[pl.ds(first, 8)].astype(BF)

    def masked(block, weight):
        return (block.astype(F32) * weight).astype(BF).reshape(4, 16, LANES)

    for g in range(EARLY):
        convert(g)
    for m in range(4):
        weight = mask_ref[m, w // 2].astype(F32)
        sb[0, pl.ds((m // 2) * 4, 4), m % 2, core] = masked(xb[w * 4 + m], weight)
    pl.semaphore_wait(barrier, DEPTH - 1 + 1 + 2 * NEAR)
    tell(1)

    my_lanes = pl.ds(pl.multiple_of(z * LANES, LANES), LANES)

    def deep_send(g, cores=slice(None)):
        place = ab.at[g, :, cores, :, my_lanes]
        for k in Z_ORDER:
            there = lax.rem(z + k, DEPTH)
            pltpu.make_async_remote_copy(
                sb.at[g, there, :, cores], place, a_send, a_recv.at[g],
                device_id=(w, there), device_id_type=MESH,
            ).start()
        pltpu.make_async_copy(sb.at[g, z, :, cores], place, a_recv.at[g]).start()

    deep_send(0, pl.ds(core, 1))

    my_rows = pl.ds(pl.multiple_of(w * 32, 32), 32)

    def metric_start():
        pltpu.make_async_copy(metric_ref.at[my_rows], mb.at[w, :, my_lanes], mz_recv).start()
        for k in Z_ORDER:
            pltpu.make_async_remote_copy(
                metric_ref.at[my_rows], mb.at[w, :, my_lanes], mz_send, mz_recv,
                device_id=(w, lax.rem(z + k, DEPTH)), device_id_type=MESH,
            ).start()

    def plane_send(g, dc):
        dx, dy = OFFSETS[g]
        there = chip_at(dx, dy) * 2 + lax.rem(core + dc, 2)
        pltpu.make_async_remote_copy(
            xb.at[pl.ds(there * 4, 4)], rb.at[g, core], s1_send, s1_recv.at[g, core],
            device_id=(there, z), device_id_type=MESH,
        ).start()

    def metric_send(g):
        dx, dy = OFFSETS[g]
        pltpu.make_async_remote_copy(
            mb.at[w], mb.at[w], mm_send, mm_recv.at[g],
            device_id=(chip_at(dx, dy) * 2 + core, z), device_id_type=MESH,
        ).start()

    def metric_across(source):
        pltpu.make_async_remote_copy(
            mb.at[source], mb.at[source], mc_send, mc_recv,
            device_id=(w + 1 - 2 * core, z), device_id_type=MESH,
        ).start()

    def screen(g, dc):
        dx, dy = OFFSETS[g]
        chip = chip_at(-dx, -dy)
        c = lax.rem(core + dc, 2)
        arrived = rb.at[g, c]
        pltpu.make_async_copy(arrived, arrived, s1_recv.at[g, c]).wait()
        for m in range(4):
            weight = mask_ref[m, chip].astype(F32)
            sb[g, pl.ds((m // 2) * 4, 4), m % 2, c] = masked(rb[g, c, m], weight)

    def core_send(g, dc):
        deep_send(g, pl.ds(lax.rem(core + dc, 2), 1))

    def metric_arrived(k):
        dx, dy = OFFSETS[k]
        source = chip_at(-dx, -dy) * 2 + core
        pltpu.make_async_copy(mb.at[source], mb.at[source], mm_recv.at[k]).wait()
        metric_across(source)

    units = [(g, dc) for dc in (0, 1) for g in range(1, NEAR + 1)]
    units_all = list(units)
    pending = []
    plane_send(0, 1)
    for g, dc in units:
        plane_send(g, dc)
    metric_start()
    screen(0, 1)
    for g in range(NEAR + 1, CHIPS):
        if g >= EARLY:
            convert(g)
        if g in FURTHER:
            r = FURTHER.index(g) + 1
            hear(r)
            if r < len(FURTHER):
                tell(r + 1)
        plane_send(g, 0)
        plane_send(g, 1)
        if g == NEAR + 1:
            core_send(0, 1)
        if g == METRIC_FROM:
            pltpu.make_async_copy(mb.at[w], mb.at[w], mz_recv).wait()
            metric_across(w)
        if g > METRIC_FROM:
            metric_send(g - METRIC_FROM)
        if g > UNITS_FROM and units:
            screen(*units.pop(0))
            pending.append(units_all.pop(0))
            if len(pending) > 1:
                core_send(*pending.pop(0))
    for g in range(CHIPS - METRIC_FROM, CHIPS):
        metric_send(g)
    for unit in units:
        screen(*unit)
        pending.append(unit)
        core_send(*pending.pop(0))
    for g in range(NEAR + 1, CHIPS):
        screen(g, 0)
        screen(g, 1)
        if g == NEAR + 1:
            core_send(*pending.pop(0))
        else:
            deep_send(g - 1)
        if g > METRIC_FROM:
            metric_arrived(g - METRIC_FROM)
    deep_send(CHIPS - 1)
    for k in range(CHIPS - METRIC_FROM, CHIPS):
        metric_arrived(k)
    pltpu.make_async_copy(mb.at[pl.ds(0, CHIPS)], mb.at[pl.ds(0, CHIPS)], mc_recv).wait()

    dxs = [dx % SIDE for dx, _ in OFFSETS]
    dys = [dy % SIDE for _, dy in OFFSETS]

    def result_send(g):
        xs = lax.rem(xx - pick(g, dxs) + SIDE, SIDE)
        ys = lax.rem(yy - pick(g, dys) + SIDE, SIDE)
        place = ob.at[pl.ds(half * 2, 2), ys, xs, :, quarter]
        pltpu.make_async_copy(yb.at[g, :, :, :, my_lanes], place, b_recv.at[g]).start()
        for k in Z_ORDER:
            there = lax.rem(z + k, DEPTH)
            lanes = pl.ds(pl.multiple_of(there * LANES, LANES), LANES)
            pltpu.make_async_remote_copy(
                yb.at[g, :, :, :, lanes], place, b_send, b_recv.at[g],
                device_id=(w, there), device_id_type=MESH,
            ).start()

    def contract(step):
        for i in range(PAIR):
            g = step * PAIR + i
            pltpu.make_async_copy(ab.at[g], ab.at[g], a_recv.at[g]).wait()
        rows = ab[pl.ds(step * PAIR, PAIR)].reshape(PAIR * 64, 1024)
        product = jnp.dot(rows, mb[...].reshape(1024, 1024), preferred_element_type=F32)
        yb[pl.ds(step * PAIR, PAIR)] = product.astype(BF).reshape(PAIR, 2, 2, 16, 1024)

    contract(0)

    @pl.loop(1, CHIPS // PAIR)
    def _(step):
        contract(step)
        for i in range(PAIR):
            result_send((step - 1) * PAIR + i)

    for i in range(PAIR):
        result_send(CHIPS - PAIR + i)

    def drain(ref, sem):
        pltpu.make_async_copy(ref, ref, sem).wait()

    drain(xb.at[pl.ds(0, 124)], s1_send)
    drain(mb.at[0, :, pl.ds(0, 7 * LANES)], mz_send)
    drain(mb.at[pl.ds(0, 15)], mm_send)
    drain(mb.at[pl.ds(0, 16)], mc_send)
    drain(sb.at[:, pl.ds(0, 7)], a_send)
    drain(yb.at[:, :, :, :, pl.ds(0, 7 * LANES)], b_send)

    @pl.loop(0, CHIPS)
    def _(g):
        xs = lax.rem(xx - pick(g, dxs) + SIDE, SIDE)
        ys = lax.rem(yy - pick(g, dys) + SIDE, SIDE)
        landed = ob.at[:, ys, xs]
        pltpu.make_async_copy(landed, landed, b_recv.at[g]).wait()
        out_ref[:, ys, xs] = landed[...].astype(F32)


def per_device(three_centre, screen_mask, metric):
    dma = pltpu.SemaphoreType.DMA
    result = pl.pallas_call(
        body,
        out_shape=pltpu.VMEM((4, SIDE, SIDE, CORES, 4, 16, LANES), F32),
        in_specs=[
            pl.BlockSpec(memory_space=pl.ANY),
            pl.BlockSpec(memory_space=pltpu.SMEM),
            pl.BlockSpec(memory_space=pl.ANY),
        ],
        out_specs=pl.BlockSpec(memory_space=pltpu.VMEM),
        scratch_shapes=[
            pltpu.VMEM((4, SIDE, SIDE, CORES, 4, 16, LANES), BF),
            pltpu.VMEM((128, 64, LANES), F32),
            pltpu.VMEM((128, 64, LANES), BF),
            pltpu.VMEM((CHIPS, CORES, 4, 64, LANES), BF),
            pltpu.VMEM((CHIPS, DEPTH, 2, 2, 16, LANES), BF),
            pltpu.VMEM((CHIPS, 2, 2, 16, 1024), BF),
            pltpu.VMEM((WIDE, 32, 1024), BF),
            pltpu.VMEM((CHIPS, 2, 2, 16, 1024), BF),
            dma((CHIPS,)), dma, dma, dma((CHIPS, CORES)), dma, dma((CHIPS,)), dma, dma((CHIPS,)),
            dma, dma, dma, dma((CHIPS,)), dma, dma,
            pltpu.SemaphoreType.REGULAR((3,)),
        ],
        compiler_params=pltpu.CompilerParams(
            collective_id=0, has_side_effects=True, vmem_limit_bytes=56 * 1024 * 1024
        ),
        name="screen_contract",
    )(three_centre, screen_mask.reshape(4, 16), metric)
    return result.reshape(4, 2048, LANES)


def solution(mesh):
    in_specs = (P(None, "wide", "narrow"), P("wide", None, "narrow"), P(None, "narrow"))
    out_specs = P("wide", None, "narrow")
    return jax.shard_map(
        per_device, mesh=mesh, in_specs=in_specs, out_specs=out_specs, check_vma=False
    )
```

```python
import jax
import jax.numpy as jnp
from jax import lax
from jax.experimental import pallas as pl
from jax.experimental.pallas import tpu as pltpu
from jax.sharding import PartitionSpec as P

MESH = pl.DeviceIdType.MESH
BF = jnp.bfloat16
F32 = jnp.float32
SIDE, CORES, DEPTH = 4, 2, 8
WIDE = SIDE * SIDE * CORES
CHIPS = SIDE * SIDE
LANES = 128
PAIR = 2

OFFSETS = (
    (0, 0), (1, 0), (-1, 0), (0, 1), (0, -1), (1, 1), (-1, -1), (-1, 1),
    (1, -1), (2, 0), (0, 2), (2, 1), (1, 2), (2, -1), (-1, 2), (2, 2),
)
Z_ORDER = (4, 3, 5, 2, 6, 1, 7)
METRIC_FROM = 8
NEAR = 4
FURTHER = (5, 11)
EARLY = 8
UNITS_FROM = 5


def pick(index, table):
    total = jnp.int32(0)
    for k, value in enumerate(table):
        if value:
            total = total + jnp.where(index == k, jnp.int32(value), jnp.int32(0))
    return total


def body(
    x_ref, mask_ref, metric_ref, out_ref,
    ob, xf, xb, rb, sb, ab, mb, yb,
    load_sem, own_sem, s1_send, s1_recv, a_send, a_recv, b_send, b_recv,
    mz_send, mz_recv, mm_send, mm_recv, mc_send, mc_recv, rounds,
):
    w = lax.axis_index("wide")
    z = lax.axis_index("narrow")
    core = lax.rem(w, 2)
    xx = lax.rem(w // 2, SIDE)
    yy = w // (2 * SIDE)
    half, quarter = z // 4, lax.rem(z, 4)

    def chip_at(dx, dy):
        return lax.rem(yy + dy + SIDE, SIDE) * SIDE + lax.rem(xx + dx + SIDE, SIDE)

    def load(g):
        dx, dy = OFFSETS[g]
        rows = pl.ds(chip_at(dx, dy) * 8, 8)
        return pltpu.make_async_copy(x_ref.at[rows], xf.at[rows], load_sem.at[g])

    barrier = pltpu.get_barrier_semaphore()
    for k in Z_ORDER:
        pl.semaphore_signal(
            barrier, inc=1, device_id=(w, lax.rem(z + k, DEPTH)), device_id_type=MESH
        )
    for g in range(NEAR, -1, -1):
        dx, dy = OFFSETS[g]
        for dc in (0, 1):
            if g == 0 and dc == 0:
                continue
            pl.semaphore_signal(
                barrier, inc=1,
                device_id=(chip_at(dx, dy) * 2 + lax.rem(core + dc, 2), z),
                device_id_type=MESH,
            )

    def tell(r):
        for g in range(1, NEAR + 1) if r == 1 else range(NEAR + 1, 2 * NEAR + 1):
            pl.semaphore_signal(
                rounds.at[r - 1], inc=1,
                device_id=(chip_at(*OFFSETS[g]) * 2 + core, z), device_id_type=MESH,
            )

    def hear(r):
        pl.semaphore_wait(rounds.at[r - 1], 4)

    for g in range(CHIPS):
        load(g).start()

    def convert(g):
        dx, dy = OFFSETS[g]
        first = chip_at(dx, dy) * 8
        load(g).wait()
        xb[pl.ds(first, 8)] = xf[pl.ds(first, 8)].astype(BF)

    def masked(block, weight):
        return (block.astype(F32) * weight).astype(BF).reshape(4, 16, LANES)

    for g in range(EARLY):
        convert(g)
    for m in range(4):
        weight = mask_ref[m, w // 2].astype(F32)
        sb[0, pl.ds((m // 2) * 4, 4), m % 2, core] = masked(xb[w * 4 + m], weight)
    pl.semaphore_wait(barrier, DEPTH - 1 + 1 + 2 * NEAR)
    tell(1)

    my_lanes = pl.ds(pl.multiple_of(z * LANES, LANES), LANES)

    def deep_send(g, cores=slice(None)):
        place = ab.at[g, :, cores, :, my_lanes]
        for k in Z_ORDER:
            there = lax.rem(z + k, DEPTH)
            pltpu.make_async_remote_copy(
                sb.at[g, there, :, cores], place, a_send, a_recv.at[g],
                device_id=(w, there), device_id_type=MESH,
            ).start()
        pltpu.make_async_copy(sb.at[g, z, :, cores], place, a_recv.at[g]).start()

    deep_send(0, pl.ds(core, 1))

    my_rows = pl.ds(pl.multiple_of(w * 32, 32), 32)

    def metric_start():
        pltpu.make_async_copy(metric_ref.at[my_rows], mb.at[w, :, my_lanes], mz_recv).start()
        for k in Z_ORDER:
            pltpu.make_async_remote_copy(
                metric_ref.at[my_rows], mb.at[w, :, my_lanes], mz_send, mz_recv,
                device_id=(w, lax.rem(z + k, DEPTH)), device_id_type=MESH,
            ).start()

    def plane_send(g, dc):
        dx, dy = OFFSETS[g]
        there = chip_at(dx, dy) * 2 + lax.rem(core + dc, 2)
        pltpu.make_async_remote_copy(
            xb.at[pl.ds(there * 4, 4)], rb.at[g, core], s1_send, s1_recv.at[g, core],
            device_id=(there, z), device_id_type=MESH,
        ).start()

    def metric_send(g):
        dx, dy = OFFSETS[g]
        pltpu.make_async_remote_copy(
            mb.at[w], mb.at[w], mm_send, mm_recv.at[g],
            device_id=(chip_at(dx, dy) * 2 + core, z), device_id_type=MESH,
        ).start()

    def metric_across(source):
        pltpu.make_async_remote_copy(
            mb.at[source], mb.at[source], mc_send, mc_recv,
            device_id=(w + 1 - 2 * core, z), device_id_type=MESH,
        ).start()

    def screen(g, dc):
        dx, dy = OFFSETS[g]
        chip = chip_at(-dx, -dy)
        c = lax.rem(core + dc, 2)
        arrived = rb.at[g, c]
        pltpu.make_async_copy(arrived, arrived, s1_recv.at[g, c]).wait()
        for m in range(4):
            weight = mask_ref[m, chip].astype(F32)
            sb[g, pl.ds((m // 2) * 4, 4), m % 2, c] = masked(rb[g, c, m], weight)

    def core_send(g, dc):
        deep_send(g, pl.ds(lax.rem(core + dc, 2), 1))

    def metric_arrived(k):
        dx, dy = OFFSETS[k]
        source = chip_at(-dx, -dy) * 2 + core
        pltpu.make_async_copy(mb.at[source], mb.at[source], mm_recv.at[k]).wait()
        metric_across(source)

    units = [(g, dc) for dc in (0, 1) for g in range(1, NEAR + 1)]
    units_all = list(units)
    pending = []
    plane_send(0, 1)
    for g, dc in units:
        plane_send(g, dc)
    metric_start()
    screen(0, 1)
    for g in range(NEAR + 1, CHIPS):
        if g >= EARLY:
            convert(g)
        if g in FURTHER:
            r = FURTHER.index(g) + 1
            hear(r)
            if r < len(FURTHER):
                tell(r + 1)
        plane_send(g, 0)
        plane_send(g, 1)
        if g == NEAR + 1:
            core_send(0, 1)
        if g == METRIC_FROM:
            pltpu.make_async_copy(mb.at[w], mb.at[w], mz_recv).wait()
            metric_across(w)
        if g > METRIC_FROM:
            metric_send(g - METRIC_FROM)
        if g > UNITS_FROM and units:
            screen(*units.pop(0))
            pending.append(units_all.pop(0))
            if len(pending) > 1:
                core_send(*pending.pop(0))
    for g in range(CHIPS - METRIC_FROM, CHIPS):
        metric_send(g)
    for unit in units:
        screen(*unit)
        pending.append(unit)
        core_send(*pending.pop(0))
    for g in range(NEAR + 1, CHIPS):
        screen(g, 0)
        screen(g, 1)
        if g == NEAR + 1:
            core_send(*pending.pop(0))
        else:
            deep_send(g - 1)
        if g > METRIC_FROM:
            metric_arrived(g - METRIC_FROM)
    deep_send(CHIPS - 1)
    for k in range(CHIPS - METRIC_FROM, CHIPS):
        metric_arrived(k)
    pltpu.make_async_copy(mb.at[pl.ds(0, CHIPS)], mb.at[pl.ds(0, CHIPS)], mc_recv).wait()

    dxs = [dx % SIDE for dx, _ in OFFSETS]
    dys = [dy % SIDE for _, dy in OFFSETS]

    def result_send(g):
        xs = lax.rem(xx - pick(g, dxs) + SIDE, SIDE)
        ys = lax.rem(yy - pick(g, dys) + SIDE, SIDE)
        place = ob.at[pl.ds(half * 2, 2), ys, xs, :, quarter]
        pltpu.make_async_copy(yb.at[g, :, :, :, my_lanes], place, b_recv.at[g]).start()
        for k in Z_ORDER:
            there = lax.rem(z + k, DEPTH)
            lanes = pl.ds(pl.multiple_of(there * LANES, LANES), LANES)
            pltpu.make_async_remote_copy(
                yb.at[g, :, :, :, lanes], place, b_send, b_recv.at[g],
                device_id=(w, there), device_id_type=MESH,
            ).start()

    def contract(step):
        for i in range(PAIR):
            g = step * PAIR + i
            pltpu.make_async_copy(ab.at[g], ab.at[g], a_recv.at[g]).wait()
        rows = ab[pl.ds(step * PAIR, PAIR)].reshape(PAIR * 64, 1024)
        product = jnp.dot(rows, mb[...].reshape(1024, 1024), preferred_element_type=F32)
        yb[pl.ds(step * PAIR, PAIR)] = product.astype(BF).reshape(PAIR, 2, 2, 16, 1024)

    contract(0)

    @pl.loop(1, CHIPS // PAIR)
    def _(step):
        contract(step)
        for i in range(PAIR):
            result_send((step - 1) * PAIR + i)

    for i in range(PAIR):
        result_send(CHIPS - PAIR + i)

    def drain(ref, sem):
        pltpu.make_async_copy(ref, ref, sem).wait()

    drain(xb.at[pl.ds(0, 124)], s1_send)
    drain(mb.at[0, :, pl.ds(0, 7 * LANES)], mz_send)
    drain(mb.at[pl.ds(0, 15)], mm_send)
    drain(mb.at[pl.ds(0, 16)], mc_send)
    drain(sb.at[:, pl.ds(0, 7)], a_send)
    drain(yb.at[:, :, :, :, pl.ds(0, 7 * LANES)], b_send)

    @pl.loop(0, CHIPS)
    def _(g):
        xs = lax.rem(xx - pick(g, dxs) + SIDE, SIDE)
        ys = lax.rem(yy - pick(g, dys) + SIDE, SIDE)
        landed = ob.at[:, ys, xs]
        pltpu.make_async_copy(landed, landed, b_recv.at[g]).wait()
        out_ref[:, ys, xs] = landed[...].astype(F32)


def per_device(three_centre, screen_mask, metric):
    dma = pltpu.SemaphoreType.DMA
    result = pl.pallas_call(
        body,
        out_shape=pltpu.VMEM((4, SIDE, SIDE, CORES, 4, 16, LANES), F32),
        in_specs=[
            pl.BlockSpec(memory_space=pl.ANY),
            pl.BlockSpec(memory_space=pltpu.SMEM),
            pl.BlockSpec(memory_space=pl.ANY),
        ],
        out_specs=pl.BlockSpec(memory_space=pltpu.VMEM),
        scratch_shapes=[
            pltpu.VMEM((4, SIDE, SIDE, CORES, 4, 16, LANES), BF),
            pltpu.VMEM((128, 64, LANES), F32),
            pltpu.VMEM((128, 64, LANES), BF),
            pltpu.VMEM((CHIPS, CORES, 4, 64, LANES), BF),
            pltpu.VMEM((CHIPS, DEPTH, 2, 2, 16, LANES), BF),
            pltpu.VMEM((CHIPS, 2, 2, 16, 1024), BF),
            pltpu.VMEM((WIDE, 32, 1024), BF),
            pltpu.VMEM((CHIPS, 2, 2, 16, 1024), BF),
            dma((CHIPS,)), dma, dma, dma((CHIPS, CORES)), dma, dma((CHIPS,)), dma, dma((CHIPS,)),
            dma, dma, dma, dma((CHIPS,)), dma, dma,
            pltpu.SemaphoreType.REGULAR((2,)),
        ],
        compiler_params=pltpu.CompilerParams(
            collective_id=0, has_side_effects=True, vmem_limit_bytes=56 * 1024 * 1024
        ),
        name="screen_contract",
    )(three_centre, screen_mask.reshape(4, 16), metric)
    return result.reshape(4, 2048, LANES)


def solution(mesh):
    in_specs = (P(None, "wide", "narrow"), P("wide", None, "narrow"), P(None, "narrow"))
    out_specs = P("wide", None, "narrow")
    return jax.shard_map(
        per_device, mesh=mesh, in_specs=in_specs, out_specs=out_specs, check_vma=False
    )
```
